32 devices in a mesh: bins: 16 (over z, y, x), diag: 2 (over core).
Axes of the slice: x: 2, y: 2, z: 4, core: 2. Of those that a mesh axis runs over, the one named last changes fastest.
Arguments:
- held_tiles: float32 [32, 2, 1024, 1024], P('bins', 'diag'), may hold values from 0.01 to 20, as said below
- placed: int32 [32], P('bins'), may hold values from 0 to 1, as said below
- bin_mask: int32 [32768], P('bins'), may hold values 0 or 1
- bias: float32 [32768], P('bins'), may hold values from 0.5 to 2
Outputs:
- balanced: float32 [32, 2, 1024, 1024], P('bins', 'diag')
- bias_out: float32 [32768], P('bins')
The draws below stay inside these ranges and needn't reach their ends.
Inputs may be any that keep to these rules, and one draw needn't show every extreme that they name: placed[q] equals placed[(q + 16) mod 32]; placed[q] is 1 where q is a multiple of 2. `held_tiles`: entries are positive.
All inputs are finite; a program needn't handle non-finite values. No bound on the sum of `bin_mask` on one device may be relied on, other than what follows from the above.
Results may differ from the reference program's by a relative error of at most 0.00012.
Values sent between devices are 32-bit elements; how exact they have to be, the bound alone decides.
A program may use at most 128 MiB of HBM per device.

```python
import math
import jax
import jax.numpy as jnp

TILE = 1024
TILES_DEV = 2
ITERS = 2
TILE_ROWS = 32
BINS = 32768


def draw_placed(key, part):
    half_flags = jax.random.randint(jax.random.fold_in(key, 11), (TILE_ROWS // 2,), 0, 2).astype(jnp.int32)
    first_rows = jnp.arange(TILE_ROWS // 2, dtype=jnp.int32) % TILES_DEV == 0
    half_flags = jnp.where(first_rows, 1, half_flags).astype(jnp.int32)
    return jnp.concatenate([half_flags, half_flags])


def draw_held_tiles(key, part):
    lines = jnp.arange(TILE, dtype=jnp.float32)
    offsets = jnp.arange(2, dtype=jnp.float32)
    distance = jnp.abs(offsets[:, None, None] * TILE + lines[None, None, :] - lines[None, :, None])
    decay = 1.0 / (1.0 + distance / 256.0)
    position = jnp.arange(TILE_ROWS, dtype=jnp.float32) / max(TILE_ROWS - 1, 1)
    shape = (TILE_ROWS, 2, TILE, TILE)
    noise = jnp.exp(jax.random.uniform(jax.random.fold_in(key, 22), shape, jnp.float32, -1.0, 1.0))
    rise = 1.0 + 2.0 * position
    return (noise * decay[None] * rise[:, None, None, None]).astype(jnp.float32)


def plant(drawn, stream_key, smallest, high):
    index_at = [jax.random.randint(jax.random.fold_in(stream_key, axis), (), 0, length) for axis, length in enumerate(drawn.shape)]
    longest = drawn.shape.index(max(drawn.shape))
    neighbour = index_at[:longest] + [(index_at[longest] + 1) % drawn.shape[longest]] + index_at[longest + 1:]
    return drawn.at[tuple(index_at)].set(smallest).at[tuple(neighbour)].set(high)


def block_scale(rng, extent, cuts, least, high):
    factor_of, own = 1.0, jax.random.fold_in(rng, 6)
    for axis_at, blocks in cuts:
        heights = jnp.exp(jax.random.uniform(jax.random.fold_in(own, axis_at), (blocks,), jnp.float32, least / len(cuts), high / len(cuts)))
        factor_of = factor_of * jnp.repeat(heights, extent[axis_at] // blocks).reshape([-1 if axis == axis_at else 1 for axis in range(len(extent))])
    return factor_of


def setup_inputs(seed: int = 0) -> dict:
    seeds = jax.random.split(jax.random.key(seed), 5)
    return {
        "held_tiles": draw_held_tiles(jax.random.fold_in(seeds[4], 71), 0),
        "placed": draw_placed(jax.random.fold_in(seeds[4], 71), 0),
        "bin_mask": plant((jax.random.randint(seeds[2], (BINS,), 0, 10) < 9).astype(jnp.int32), jax.random.fold_in(seeds[2], 1), 0, 1),
        "bias": jnp.clip(jnp.exp(math.log(2.0) - 1.3862944 * jax.random.uniform(seeds[3], (BINS,), jnp.float32) ** block_scale(seeds[3], (BINS,), ((0, 16),), -0.2, 0.2)), 0.5, 2.0),
    }


def reference(held_tiles, placed, bin_mask, bias):
    row_index = jnp.arange(TILE_ROWS, dtype=jnp.int32)
    partner = (row_index + TILE_ROWS // 2) % TILE_ROWS
    source = jnp.where(placed == 1, partner, row_index).astype(jnp.int32)
    home_tiles = held_tiles[source]
    live = bin_mask.astype(jnp.float32).reshape(TILE_ROWS, TILE)
    empty_row = jnp.zeros((1, TILE), jnp.float32)
    live_next = jnp.concatenate([live[1:], empty_row], axis=0)
    lines = jnp.arange(TILE, dtype=jnp.int32)
    upper_mask = (lines[:, None] <= lines[None, :]).astype(jnp.float32)
    diag_block = home_tiles[:, 0] * upper_mask * live[:, :, None] * live[:, None, :]
    off_block = home_tiles[:, 1] * live[:, :, None] * live_next[:, None, :]
    bias_now = bias.reshape(TILE_ROWS, TILE)
    for repeat in range(ITERS):
        row_diag = jnp.sum(diag_block, axis=2)
        col_diag = jnp.sum(diag_block, axis=1) - jnp.diagonal(diag_block, axis1=1, axis2=2)
        row_off = jnp.sum(off_block, axis=2)
        col_off = jnp.sum(off_block, axis=1)
        sums = row_diag + col_diag + row_off + jnp.concatenate([empty_row, col_off[:-1]], axis=0)
        masked_total = jnp.sum(sums * live)
        live_count = jnp.sum(live)
        mean_sum = masked_total / live_count
        factor = jnp.where(live > 0, sums / mean_sum, 1.0)
        bias_now = bias_now * factor
        inverse = 1.0 / factor
        inverse_next = jnp.concatenate([inverse[1:], empty_row], axis=0)
        diag_block = diag_block * inverse[:, :, None] * inverse[:, None, :]
        off_block = off_block * inverse[:, :, None] * inverse_next[:, None, :]
    balanced = jnp.stack([diag_block, off_block], axis=1)
    return balanced, bias_now.reshape(BINS)
```

```python
import functools

import jax
import jax.numpy as jnp
from jax import lax
from jax.experimental import pallas as pl
from jax.experimental.pallas import tpu as pltpu
from jax.sharding import PartitionSpec as P

ITERS = 2
B = 128
MESH = pl.DeviceIdType.MESH
F32 = jnp.float32


def kernel(n, rows_dev, size, held, placed, mask, bias, tiles_out, u_out, v_out, bias_out,
           home, recv, live_col, next_mask, row, col_acc, diag_vec, contrib, pair, edge_in, edge_out, nxt, tot,
           in_sem, out_sem, send_sem, recv_sem, mask_sem, pair_sem, edge_sem, next_sem, tot_sem):
    b, d = lax.axis_index("bins"), lax.axis_index("diag")
    count = n * 2
    me = b * 2 + d
    on_diag, off_diag = d == 0, d == 1
    has_prev, has_next = b > 0, b < n - 1
    strips = size // B
    width = rows_dev * size
    half = n // 2
    partner = (lax.rem(b + half, n), d)

    barrier = pltpu.get_barrier_semaphore()

    def other(off):
        target = lax.rem(me + off, count)
        return (target // 2, lax.rem(target, 2))

    def greet(off, carry):
        pl.semaphore_signal(barrier, inc=1, device_id=other(off), device_id_type=MESH)
        return carry

    lax.fori_loop(1, count, greet, 0)
    loads = []
    for t in range(rows_dev):
        loads.append(pltpu.make_async_copy(held.at[t, 0], home.at[t], in_sem.at[t]))
        loads[-1].start()
    pl.semaphore_wait(barrier, count - 1)

    mask_send = pltpu.make_async_remote_copy(
        mask.at[:, :size], next_mask, mask_sem.at[0], mask_sem.at[1], device_id=(jnp.maximum(b - 1, 0), 1), device_id_type=MESH)

    @pl.when(on_diag & has_prev)
    def _():
        mask_send.start()

    def piece(t, r, first):
        part = (t, pl.ds(r * B, B), pl.ds(first, size - first))
        return pltpu.make_async_remote_copy(
            held.at[t, 0, part[1], part[2]], recv.at[part], send_sem.at[t, r], recv_sem.at[t, r],
            device_id=partner, device_id_type=MESH)

    order = [(t, r) for t in range(rows_dev) for r in range(strips)]

    @pl.when(on_diag)
    def _():
        for t, r in order:
            piece(t, r, r * B).start()

    @pl.when(off_diag)
    def _():
        for t, r in order:
            piece(t, r, 0).start()

    @pl.when(off_diag & has_next)
    def _():
        mask_send.wait_recv()

    @pl.when(on_diag & has_prev)
    def _():
        mask_send.wait_send()

    live = mask[...].astype(F32)
    after = jnp.where(has_next, next_mask[...].astype(F32), 0.0)
    live_col[:, width - size:] = jnp.where(on_diag, live[:, width - size:], after)
    if rows_dev > 1:
        live_col[:, :width - size] = jnp.where(on_diag, live[:, :width - size], live[:, size:])
    for t in range(rows_dev):
        loads[t].wait()
    col_acc[...] = jnp.zeros_like(col_acc)
    line = lax.broadcasted_iota(jnp.int32, (B, B), 0)
    lane = lax.broadcasted_iota(jnp.int32, (B, B), 1)
    shift = jnp.where(on_diag, 0, -2 * size)

    def down(vector):
        return jnp.broadcast_to(vector, (B, B)).T

    def folded(block):
        return jnp.sum(block.reshape(B // 8, 8, B), axis=0)

    def lanes(c):
        return pl.ds(pl.multiple_of(c * B, B), B)

    def out_copy(t, r):
        return pltpu.make_async_copy(home.at[t, pl.ds(r * B, B)], tiles_out.at[t, pl.ds(r * B, B)], out_sem.at[t, r])

    for t, r in order:
        @pl.when(on_diag)
        def _():
            piece(t, r, r * B).wait_recv()

        @pl.when(off_diag)
        def _():
            piece(t, r, 0).wait_recv()

        spot = pl.ds(t * size + r * B, B)
        live_down = down(mask[:, spot].astype(F32))
        moved = jnp.broadcast_to(placed[t], (B, B)) == 1

        def first_pass(c, total):
            at = (t, pl.ds(r * B, B), lanes(c))
            block = jnp.where(moved, recv[at], home[at])
            keep = line + (r * B + shift) <= lane + c * B
            across = live_col[:, pl.ds(pl.multiple_of(t * size + c * B, B), B)]
            block = jnp.where(keep, block, 0.0) * live_down * across
            home[at] = block
            col_acc[t, :, lanes(c)] += folded(block)
            return total + block

        total = lax.fori_loop(0, strips, first_pass, jnp.zeros((B, B), F32))
        row[:, spot] = jnp.sum(total.T, axis=0, keepdims=True)
        corner = home[t, pl.ds(r * B, B), pl.ds(r * B, B)]
        corner = jnp.sum(jnp.where(line == lane, corner, 0.0), axis=0, keepdims=True)
        diag_vec[:, spot] = jnp.where(on_diag, corner, 0.0)
        out_copy(t, r).start()

    u_out[...] = jnp.ones_like(u_out)
    v_out[...] = jnp.ones_like(v_out)
    bias_out[...] = bias[...]
    first_lane = lax.broadcasted_iota(jnp.int32, (1, B), 1)

    for k in range(ITERS):
        if k > 0:
            col_acc[...] = jnp.zeros_like(col_acc)
            for t in range(rows_dev):
                def strip_pass(r, carry):
                    spot = pl.ds(pl.multiple_of(t * size + r * B, B), B)
                    u_down = down(u_out[:, spot])

                    def later_pass(c, total):
                        block = home[t, lanes(r), lanes(c)]
                        col_acc[t, :, lanes(c)] += folded(block * u_down)
                        return total + block * v_out[:, pl.ds(pl.multiple_of(t * size + c * B, B), B)]

                    total = lax.fori_loop(0, strips, later_pass, jnp.zeros((B, B), F32))
                    row[:, spot] = jnp.sum(total.T, axis=0, keepdims=True)
                    return carry

                lax.fori_loop(0, strips, strip_pass, 0)
        cols = jnp.concatenate([jnp.sum(col_acc[t], axis=0, keepdims=True) for t in range(rows_dev)], axis=1) * v_out[...]
        rows = row[...] * u_out[...]
        corner = diag_vec[...] * u_out[...] * v_out[...]
        zero = jnp.zeros((1, size), F32)
        moved_cols = jnp.concatenate([zero, cols[:, :width - size]], axis=1)
        mine = rows + jnp.where(on_diag, cols - corner, moved_cols)
        edge = jnp.where(on_diag, 0.0, cols[:, width - size:])
        contrib[k] = mine
        edge_out[k] = edge
        partial = jnp.sum(mine) + jnp.sum(edge)
        kept = jnp.where(on_diag, jnp.sum(mask[...].astype(F32)), 0.0)
        tot[k, me] = jnp.where(first_lane == 0, partial, jnp.where(first_lane == 1, kept, 0.0))

        def tot_copy(off):
            return pltpu.make_async_remote_copy(
                tot.at[k, me], tot.at[k, me], tot_sem.at[k, 0], tot_sem.at[k, 1], device_id=other(off), device_id_type=MESH)

        def tot_start(off, carry):
            tot_copy(off).start()
            return carry

        to_pair = pltpu.make_async_remote_copy(
            contrib.at[k], pair.at[k], pair_sem.at[k, 0], pair_sem.at[k, 1], device_id=(b, 1 - d), device_id_type=MESH)
        to_edge = [pltpu.make_async_remote_copy(
            edge_out.at[k], edge_in.at[k], edge_sem.at[k, i], edge_sem.at[k, 2],
            device_id=(jnp.minimum(b + 1, n - 1), i), device_id_type=MESH) for i in range(2)]
        to_prev = [pltpu.make_async_remote_copy(
            contrib.at[k, :, :size], nxt.at[k, i], next_sem.at[k, 0], next_sem.at[k, 1 + i],
            device_id=(jnp.maximum(b - 1, 0), 1), device_id_type=MESH) for i in range(2)]

        @pl.when(off_diag & has_next)
        def _():
            for copy in to_edge:
                copy.start()

        for i in range(2):
            @pl.when((d == i) & has_prev)
            def _():
                to_prev[i].start()

        lax.fori_loop(1, count, tot_start, 0)
        to_pair.start()
        to_pair.wait()

        @pl.when(off_diag & has_next)
        def _():
            for copy in to_edge:
                copy.wait_send()
            for copy in to_prev:
                copy.wait_recv()

        @pl.when(has_prev)
        def _():
            to_edge[0].wait_recv()
            to_prev[0].wait_send()

        many = tot.at[k, pl.ds(0, count - 1)]
        pltpu.make_async_copy(many, many, tot_sem.at[k, 0]).wait()
        pltpu.make_async_copy(many, many, tot_sem.at[k, 1]).wait()

        both = jnp.sum(tot[k], axis=0)
        mean = jnp.sum(jnp.where(first_lane == 0, both, 0.0), axis=1, keepdims=True) / jnp.sum(
            jnp.where(first_lane == 1, both, 0.0), axis=1, keepdims=True)
        mine, theirs = contrib[k], pair[k]
        sums = jnp.where(on_diag, mine, theirs) + jnp.where(on_diag, theirs, mine)
        arrived = jnp.where(has_prev, edge_in[k], 0.0)
        if rows_dev > 1:
            arrived = jnp.concatenate([arrived, jnp.zeros((1, width - size), F32)], axis=1)
        sums = sums + arrived
        factor = jnp.where(mask[...] > 0, sums / mean, 1.0)
        bias_out[...] = bias_out[...] * factor
        inverse = 1.0 / factor
        next_sums = nxt[k, 0] + nxt[k, 1] + edge_out[k]
        next_inverse = 1.0 / jnp.where(next_mask[...] > 0, next_sums / mean, 1.0)
        next_inverse = jnp.where(has_next, next_inverse, 0.0)
        if rows_dev > 1:
            next_inverse = jnp.concatenate([inverse[:, size:], next_inverse], axis=1)
        u_out[...] = u_out[...] * inverse
        v_out[...] = v_out[...] * jnp.where(on_diag, inverse, next_inverse)

    for t, r in order:
        out_copy(t, r).wait()

    @pl.when(on_diag)
    def _():
        for t, r in order:
            piece(t, r, r * B).wait_send()

    @pl.when(off_diag)
    def _():
        for t, r in order:
            piece(t, r, 0).wait_send()


def local(n, held_tiles, placed, bin_mask, bias):
    rows_dev, size = held_tiles.shape[0], held_tiles.shape[2]
    strips, width, count = size // B, rows_dev * size, n * 2
    flags = jnp.broadcast_to(placed[:, None, None], (rows_dev, 1, B))
    vmem, anywhere = pl.BlockSpec(memory_space=pltpu.VMEM), pl.BlockSpec(memory_space=pl.ANY)
    wide = jax.ShapeDtypeStruct((1, width), F32)
    dma = pltpu.SemaphoreType.DMA
    tiles, u, v, bias_new = pl.pallas_call(
        functools.partial(kernel, n, rows_dev, size),
        out_shape=(jax.ShapeDtypeStruct((rows_dev, size, size), F32), wide, wide, wide),
        in_specs=[anywhere, vmem, vmem, vmem],
        out_specs=(anywhere, vmem, vmem, vmem),
        scratch_shapes=[
            pltpu.VMEM((rows_dev, size, size), F32),
            pltpu.VMEM((rows_dev, size, size), F32),
            pltpu.VMEM((1, width), F32),
            pltpu.VMEM((1, size), jnp.int32),
            pltpu.VMEM((1, width), F32),
            pltpu.VMEM((rows_dev, 8, size), F32),
            pltpu.VMEM((1, width), F32),
            pltpu.VMEM((ITERS, 1, width), F32),
            pltpu.VMEM((ITERS, 1, width), F32),
            pltpu.VMEM((ITERS, 1, size), F32),
            pltpu.VMEM((ITERS, 1, size), F32),
            pltpu.VMEM((ITERS, 2, 1, size), F32),
            pltpu.VMEM((ITERS, count, 1, B), F32),
            dma((rows_dev,)),
            dma((rows_dev, strips)),
            dma((rows_dev, strips)),
            dma((rows_dev, strips)),
            dma((2,)),
            dma((ITERS, 2)),
            dma((ITERS, 3)),
            dma((ITERS, 3)),
            dma((ITERS, 2)),
        ],
        compiler_params=pltpu.CompilerParams(collective_id=0, has_side_effects=True),
    )(held_tiles, flags, bin_mask.reshape(1, width), bias.reshape(1, width))
    u, v = u.reshape(rows_dev, 1, size, 1), v.reshape(rows_dev, 1, 1, size)
    return (tiles[:, None] * u) * v, bias_new.reshape(width)


def solution(mesh):
    specs = (P("bins", "diag", None, None), P("bins"), P("bins"), P("bins"))
    return jax.shard_map(
        functools.partial(local, mesh.shape["bins"]),
        mesh=mesh,
        in_specs=specs,
        out_specs=(P("bins", "diag", None, None), P("bins")),
        check_vma=False,
    )
```

```python
import functools

import jax
import jax.numpy as jnp
from jax import lax
from jax.experimental import pallas as pl
from jax.experimental.pallas import tpu as pltpu
from jax.sharding import PartitionSpec as P

ITERS = 2
B = 128
MESH = pl.DeviceIdType.MESH
F32 = jnp.float32


def kernel(n, rows_dev, size, held, placed, mask, bias, tiles_out, u_out, v_out, bias_out,
           home, recv, live_col, next_mask, row, col_acc, diag_vec, contrib, pair, edge_in, edge_out, nxt, tot, fold_out, fold_in,
           in_sem, out_sem, send_sem, recv_sem, mask_sem, pair_sem, edge_sem, next_sem, tot_sem, fold_sem):
    b, d = lax.axis_index("bins"), lax.axis_index("diag")
    count = n * 2
    me = b * 2 + d
    on_diag, off_diag = d == 0, d == 1
    has_prev, has_next = b > 0, b < n - 1
    strips = size // B
    width = rows_dev * size
    half = n // 2
    partner = (lax.rem(b + half, n), d)

    barrier = pltpu.get_barrier_semaphore()

    def other(off):
        target = lax.rem(me + off, count)
        return (target // 2, lax.rem(target, 2))

    def greet(off, carry):
        pl.semaphore_signal(barrier, inc=1, device_id=other(off), device_id_type=MESH)
        return carry

    lax.fori_loop(1, count, greet, 0)
    loads = []
    for t in range(rows_dev):
        loads.append(pltpu.make_async_copy(held.at[t, 0], home.at[t], in_sem.at[t]))
        loads[-1].start()
    pl.semaphore_wait(barrier, count - 1)

    mask_send = pltpu.make_async_remote_copy(
        mask.at[:, :size], next_mask, mask_sem.at[0], mask_sem.at[1], device_id=(jnp.maximum(b - 1, 0), 1), device_id_type=MESH)

    @pl.when(on_diag & has_prev)
    def _():
        mask_send.start()

    def piece(t, r, first):
        part = (t, pl.ds(r * B, B), pl.ds(first, size - first))
        return pltpu.make_async_remote_copy(
            held.at[t, 0, part[1], part[2]], recv.at[part], send_sem.at[t, r], recv_sem.at[t, r],
            device_id=partner, device_id_type=MESH)

    order = [(t, r) for t in range(rows_dev) for r in range(strips)]

    def folds(t):
        return pltpu.make_async_remote_copy(
            fold_out.at[t], fold_in.at[t], fold_sem.at[t, 0], fold_sem.at[t, 1], device_id=partner, device_id_type=MESH)

    line = lax.broadcasted_iota(jnp.int32, (B, B), 0)
    lane = lax.broadcasted_iota(jnp.int32, (B, B), 1)

    @pl.when(on_diag)
    def _():
        for t, r in order:
            if r < strips - 1:
                piece(t, r, (r + 1) * B).start()

    @pl.when(off_diag)
    def _():
        for t, r in order:
            piece(t, r, 0).start()

    for t in range(rows_dev):
        loads[t].wait()

    @pl.when(on_diag)
    def _():
        for t in range(rows_dev):
            def fold(j, carry):
                low, high = [pl.ds(pl.multiple_of((2 * j + i) * B, B), B) for i in range(2)]
                even, odd = home[t, low, low], home[t, high, high]
                fold_out[t, j, :B] = jnp.where(line <= lane, even, odd.T)
                corner = jnp.sum(jnp.where(line == lane, odd, 0.0), axis=0, keepdims=True)
                fold_out[t, j, B:] = jnp.broadcast_to(corner, (8, B))
                return carry

            lax.fori_loop(0, strips // 2, fold, 0)
        for t in range(rows_dev):
            folds(t).start()

    @pl.when(off_diag & has_next)
    def _():
        mask_send.wait_recv()

    @pl.when(on_diag & has_prev)
    def _():
        mask_send.wait_send()

    live = mask[...].astype(F32)
    after = jnp.where(has_next, next_mask[...].astype(F32), 0.0)
    live_col[:, width - size:] = jnp.where(on_diag, live[:, width - size:], after)
    if rows_dev > 1:
        live_col[:, :width - size] = jnp.where(on_diag, live[:, :width - size], live[:, size:])
    col_acc[...] = jnp.zeros_like(col_acc)
    shift = jnp.where(on_diag, 0, -2 * size)

    def down(vector):
        return jnp.broadcast_to(vector, (B, B)).T

    def folded(block):
        return jnp.sum(block.reshape(B // 8, 8, B), axis=0)

    def lanes(c):
        return pl.ds(pl.multiple_of(c * B, B), B)

    def out_copy(t, r):
        return pltpu.make_async_copy(home.at[t, pl.ds(r * B, B)], tiles_out.at[t, pl.ds(r * B, B)], out_sem.at[t, r])

    for t, r in order:
        @pl.when(on_diag)
        def _():
            if r == 0:
                folds(t).wait_recv()

                def unfold(j, carry):
                    low, high = [pl.ds(pl.multiple_of((2 * j + i) * B, B), B) for i in range(2)]
                    both = fold_in[t, j, :B]
                    recv[t, low, low] = both
                    recv[t, high, high] = jnp.where(line == lane, fold_in[t, j, B:B + 1], both.T)
                    return carry

                lax.fori_loop(0, strips // 2, unfold, 0)
            if r < strips - 1:
                piece(t, r, (r + 1) * B).wait_recv()

        @pl.when(off_diag)
        def _():
            piece(t, r, 0).wait_recv()

        spot = pl.ds(t * size + r * B, B)
        live_down = down(mask[:, spot].astype(F32))
        moved = jnp.full((B, B), placed[t]) == 1

        def first_pass(c, total):
            at = (t, pl.ds(r * B, B), lanes(c))
            block = jnp.where(moved, recv[at], home[at])
            keep = line + (r * B + shift) <= lane + c * B
            across = live_col[:, pl.ds(pl.multiple_of(t * size + c * B, B), B)]
            block = jnp.where(keep, block, 0.0) * live_down * across
            home[at] = block
            col_acc[t, :, lanes(c)] += folded(block)
            return total + block

        total = lax.fori_loop(0, strips, first_pass, jnp.zeros((B, B), F32))
        row[:, spot] = jnp.sum(total.T, axis=0, keepdims=True)
        corner = home[t, pl.ds(r * B, B), pl.ds(r * B, B)]
        corner = jnp.sum(jnp.where(line == lane, corner, 0.0), axis=0, keepdims=True)
        diag_vec[:, spot] = jnp.where(on_diag, corner, 0.0)
        out_copy(t, r).start()

    u_out[...] = jnp.ones_like(u_out)
    v_out[...] = jnp.ones_like(v_out)
    bias_out[...] = bias[...]
    first_lane = lax.broadcasted_iota(jnp.int32, (1, B), 1)

    for k in range(ITERS):
        if k > 0:
            col_acc[...] = jnp.zeros_like(col_acc)
            for t in range(rows_dev):
                def strip_pass(r, carry):
                    spot = pl.ds(pl.multiple_of(t * size + r * B, B), B)
                    u_down = down(u_out[:, spot])

                    def later_pass(c, total):
                        block = home[t, lanes(r), c * B:(c + 1) * B]
                        col_acc[t, :, c * B:(c + 1) * B] += folded(block * u_down)
                        return total + block * v_out[:, t * size + c * B:t * size + (c + 1) * B]

                    total = jnp.zeros((B, B), F32)
                    for c in range(strips):
                        total = later_pass(c, total)
                    row[:, spot] = jnp.sum(total.T, axis=0, keepdims=True)
                    return carry

                lax.fori_loop(0, strips, strip_pass, 0)
        cols = jnp.concatenate([jnp.sum(col_acc[t], axis=0, keepdims=True) for t in range(rows_dev)], axis=1) * v_out[...]
        rows = row[...] * u_out[...]
        corner = diag_vec[...] * u_out[...] * v_out[...]
        zero = jnp.zeros((1, size), F32)
        moved_cols = jnp.concatenate([zero, cols[:, :width - size]], axis=1)
        mine = rows + jnp.where(on_diag, cols - corner, moved_cols)
        edge = jnp.where(on_diag, 0.0, cols[:, width - size:])
        contrib[k] = mine
        edge_out[k] = edge
        partial = jnp.sum(mine) + jnp.sum(edge)
        kept = jnp.where(on_diag, jnp.sum(mask[...].astype(F32)), 0.0)
        tot[k, me] = jnp.where(first_lane == 0, partial, jnp.where(first_lane == 1, kept, 0.0))

        def tot_copy(off):
            return pltpu.make_async_remote_copy(
                tot.at[k, me], tot.at[k, me], tot_sem.at[k, 0], tot_sem.at[k, 1], device_id=other(off), device_id_type=MESH)

        def tot_start(off, carry):
            tot_copy(off).start()
            return carry

        to_pair = pltpu.make_async_remote_copy(
            contrib.at[k], pair.at[k], pair_sem.at[k, 0], pair_sem.at[k, 1], device_id=(b, 1 - d), device_id_type=MESH)
        to_edge = [pltpu.make_async_remote_copy(
            edge_out.at[k], edge_in.at[k], edge_sem.at[k, i], edge_sem.at[k, 2],
            device_id=(jnp.minimum(b + 1, n - 1), i), device_id_type=MESH) for i in range(2)]
        to_prev = [pltpu.make_async_remote_copy(
            contrib.at[k, :, :size], nxt.at[k, i], next_sem.at[k, 0], next_sem.at[k, 1 + i],
            device_id=(jnp.maximum(b - 1, 0), 1), device_id_type=MESH) for i in range(2)]

        @pl.when(off_diag & has_next)
        def _():
            for copy in to_edge:
                copy.start()

        for i in range(2):
            @pl.when((d == i) & has_prev)
            def _():
                to_prev[i].start()

        lax.fori_loop(1, count, tot_start, 0)
        to_pair.start()
        to_pair.wait()

        @pl.when(off_diag & has_next)
        def _():
            for copy in to_edge:
                copy.wait_send()
            for copy in to_prev:
                copy.wait_recv()

        @pl.when(has_prev)
        def _():
            to_edge[0].wait_recv()
            to_prev[0].wait_send()

        many = tot.at[k, pl.ds(0, count - 1)]
        pltpu.make_async_copy(many, many, tot_sem.at[k, 0]).wait()
        pltpu.make_async_copy(many, many, tot_sem.at[k, 1]).wait()

        both = jnp.sum(tot[k], axis=0)
        mean = jnp.sum(jnp.where(first_lane == 0, both, 0.0), axis=1, keepdims=True) / jnp.sum(
            jnp.where(first_lane == 1, both, 0.0), axis=1, keepdims=True)
        mine, theirs = contrib[k], pair[k]
        sums = jnp.where(on_diag, mine, theirs) + jnp.where(on_diag, theirs, mine)
        arrived = jnp.where(has_prev, edge_in[k], 0.0)
        if rows_dev > 1:
            arrived = jnp.concatenate([arrived, jnp.zeros((1, width - size), F32)], axis=1)
        sums = sums + arrived
        factor = jnp.where(mask[...] > 0, sums / mean, 1.0)
        bias_out[...] = bias_out[...] * factor
        inverse = 1.0 / factor
        next_sums = nxt[k, 0] + nxt[k, 1] + edge_out[k]
        next_inverse = 1.0 / jnp.where(next_mask[...] > 0, next_sums / mean, 1.0)
        next_inverse = jnp.where(has_next, next_inverse, 0.0)
        if rows_dev > 1:
            next_inverse = jnp.concatenate([inverse[:, size:], next_inverse], axis=1)
        u_out[...] = u_out[...] * inverse
        v_out[...] = v_out[...] * jnp.where(on_diag, inverse, next_inverse)

    for t, r in order:
        out_copy(t, r).wait()

    @pl.when(on_diag)
    def _():
        for t, r in order:
            if r < strips - 1:
                piece(t, r, (r + 1) * B).wait_send()
        for t in range(rows_dev):
            folds(t).wait_send()

    @pl.when(off_diag)
    def _():
        for t, r in order:
            piece(t, r, 0).wait_send()


def scale(tall, tiles, u, v, out):
    for r in range(tall // B):
        spot = pl.ds(r * B, B)
        u_down = jnp.broadcast_to(u[:, spot], (B, B)).T
        for c in range(v.shape[1] // B):
            across = pl.ds(c * B, B)
            out[0, 0, spot, across] = tiles[0, spot, across] * u_down * v[:, across]


def local(n, held_tiles, placed, bin_mask, bias):
    rows_dev, size = held_tiles.shape[0], held_tiles.shape[2]
    strips, width, count = size // B, rows_dev * size, n * 2
    vmem, anywhere = pl.BlockSpec(memory_space=pltpu.VMEM), pl.BlockSpec(memory_space=pl.ANY)
    wide = jax.ShapeDtypeStruct((1, width), F32)
    dma = pltpu.SemaphoreType.DMA
    tiles, u, v, bias_new = pl.pallas_call(
        functools.partial(kernel, n, rows_dev, size),
        out_shape=(jax.ShapeDtypeStruct((rows_dev, size, size), F32), wide, wide, wide),
        in_specs=[anywhere, pl.BlockSpec(memory_space=pltpu.SMEM), vmem, vmem],
        out_specs=(anywhere, vmem, vmem, vmem),
        scratch_shapes=[
            pltpu.VMEM((rows_dev, size, size), F32),
            pltpu.VMEM((rows_dev, size, size), F32),
            pltpu.VMEM((1, width), F32),
            pltpu.VMEM((1, size), jnp.int32),
            pltpu.VMEM((1, width), F32),
            pltpu.VMEM((rows_dev, 8, size), F32),
            pltpu.VMEM((1, width), F32),
            pltpu.VMEM((ITERS, 1, width), F32),
            pltpu.VMEM((ITERS, 1, width), F32),
            pltpu.VMEM((ITERS, 1, size), F32),
            pltpu.VMEM((ITERS, 1, size), F32),
            pltpu.VMEM((ITERS, 2, 1, size), F32),
            pltpu.VMEM((ITERS, count, 1, B), F32),
            pltpu.VMEM((rows_dev, strips // 2, B + 8, B), F32),
            pltpu.VMEM((rows_dev, strips // 2, B + 8, B), F32),
            dma((rows_dev,)),
            dma((rows_dev, strips)),
            dma((rows_dev, strips)),
            dma((rows_dev, strips)),
            dma((2,)),
            dma((ITERS, 2)),
            dma((ITERS, 3)),
            dma((ITERS, 3)),
            dma((ITERS, 2)),
            dma((rows_dev, 2)),
        ],
        compiler_params=pltpu.CompilerParams(collective_id=0, has_side_effects=True),
    )(held_tiles, placed, bin_mask.reshape(1, width), bias.reshape(1, width))
    tall = 4 * B
    balanced = pl.pallas_call(
        functools.partial(scale, tall),
        grid=(rows_dev, size // tall),
        out_shape=jax.ShapeDtypeStruct((rows_dev, 1, size, size), F32),
        in_specs=[
            pl.BlockSpec((1, tall, size), lambda t, s: (t, s, 0)),
            pl.BlockSpec((1, tall), lambda t, s: (0, t * (size // tall) + s)),
            pl.BlockSpec((1, size), lambda t, s: (0, t)),
        ],
        out_specs=pl.BlockSpec((1, 1, tall, size), lambda t, s: (t, 0, s, 0)),
    )(tiles, u, v)
    return balanced, bias_new.reshape(width)


def solution(mesh):
    specs = (P("bins", "diag", None, None), P("bins"), P("bins"), P("bins"))
    return jax.shard_map(
        functools.partial(local, mesh.shape["bins"]),
        mesh=mesh,
        in_specs=specs,
        out_specs=(P("bins", "diag", None, None), P("bins")),
        check_vma=False,
    )
```

```python
import functools

import jax
import jax.numpy as jnp
from jax import lax
from jax.experimental import pallas as pl
from jax.experimental.pallas import tpu as pltpu
from jax.sharding import PartitionSpec as P

ITERS = 2
B = 128
MESH = pl.DeviceIdType.MESH
F32 = jnp.float32


def kernel(n, rows_dev, size, held, placed, mask, bias, tiles_out, u_out, v_out, bias_out,
           home, recv, live_col, next_mask, row, col_acc, diag_vec, contrib, pair, edge_in, edge_out, nxt, tot, fold_out, fold_in, sums_now,
           in_sem, out_sem, send_sem, recv_sem, mask_sem, pair_sem, edge_sem, next_sem, tot_sem, fold_sem):
    b, d = lax.axis_index("bins"), lax.axis_index("diag")
    count = n * 2
    me = b * 2 + d
    on_diag, off_diag = d == 0, d == 1
    has_prev, has_next = b > 0, b < n - 1
    strips = size // B
    width = rows_dev * size
    half = n // 2
    partner = (lax.rem(b + half, n), d)

    barrier = pltpu.get_barrier_semaphore()

    def other(off):
        target = lax.rem(me + off, count)
        return (target // 2, lax.rem(target, 2))

    def greet(off, carry):
        pl.semaphore_signal(barrier, inc=1, device_id=other(off), device_id_type=MESH)
        return carry

    lax.fori_loop(1, count, greet, 0)
    loads = []
    for t in range(rows_dev):
        loads.append(pltpu.make_async_copy(held.at[t, 0], home.at[t], in_sem.at[t]))
        loads[-1].start()
    pl.semaphore_wait(barrier, count - 1)

    mask_send = pltpu.make_async_remote_copy(
        mask.at[:, :size], next_mask, mask_sem.at[0], mask_sem.at[1], device_id=(jnp.maximum(b - 1, 0), 1), device_id_type=MESH)

    @pl.when(on_diag & has_prev)
    def _():
        mask_send.start()

    def piece(t, r, first):
        part = (t, pl.ds(r * B, B), pl.ds(first, size - first))
        return pltpu.make_async_remote_copy(
            held.at[t, 0, part[1], part[2]], recv.at[part], send_sem.at[t, r], recv_sem.at[t, r],
            device_id=partner, device_id_type=MESH)

    order = [(t, r) for t in range(rows_dev) for r in range(strips)]

    def folds(t):
        return pltpu.make_async_remote_copy(
            fold_out.at[t], fold_in.at[t], fold_sem.at[t, 0], fold_sem.at[t, 1], device_id=partner, device_id_type=MESH)

    line = lax.broadcasted_iota(jnp.int32, (B, B), 0)
    lane = lax.broadcasted_iota(jnp.int32, (B, B), 1)

    @pl.when(on_diag)
    def _():
        for t, r in order:
            if r < strips - 1:
                piece(t, r, (r + 1) * B).start()

    @pl.when(off_diag)
    def _():
        for t, r in order:
            piece(t, r, 0).start()

    for t in range(rows_dev):
        loads[t].wait()

    @pl.when(on_diag)
    def _():
        for t in range(rows_dev):
            def fold(j, carry):
                low, high = [pl.ds(pl.multiple_of((2 * j + i) * B, B), B) for i in range(2)]
                even, odd = home[t, low, low], home[t, high, high]
                fold_out[t, j, :B] = jnp.where(line <= lane, even, odd.T)
                corner = jnp.sum(jnp.where(line == lane, odd, 0.0), axis=0, keepdims=True)
                fold_out[t, j, B:] = jnp.broadcast_to(corner, (8, B))
                return carry

            lax.fori_loop(0, strips // 2, fold, 0)
        for t in range(rows_dev):
            folds(t).start()

    @pl.when(off_diag & has_next)
    def _():
        mask_send.wait_recv()

    @pl.when(on_diag & has_prev)
    def _():
        mask_send.wait_send()

    live = mask[...].astype(F32)
    after = jnp.where(has_next, next_mask[...].astype(F32), 0.0)
    live_col[:, width - size:] = jnp.where(on_diag, live[:, width - size:], after)
    if rows_dev > 1:
        live_col[:, :width - size] = jnp.where(on_diag, live[:, :width - size], live[:, size:])
    col_acc[...] = jnp.zeros_like(col_acc)
    shift = jnp.where(on_diag, 0, -2 * size)

    def down(vector):
        return jnp.broadcast_to(vector, (B, B)).T

    def folded(block):
        return jnp.sum(block.reshape(B // 8, 8, B), axis=0)

    def lanes(c):
        return pl.ds(pl.multiple_of(c * B, B), B)

    def out_copy(t, r):
        return pltpu.make_async_copy(home.at[t, pl.ds(r * B, B)], tiles_out.at[t, pl.ds(r * B, B)], out_sem.at[t, r])

    for t, r in order:
        @pl.when(on_diag)
        def _():
            if r == 0:
                folds(t).wait_recv()

                def unfold(j, carry):
                    low, high = [pl.ds(pl.multiple_of((2 * j + i) * B, B), B) for i in range(2)]
                    both = fold_in[t, j, :B]
                    recv[t, low, low] = both
                    recv[t, high, high] = jnp.where(line == lane, fold_in[t, j, B:B + 1], both.T)
                    return carry

                lax.fori_loop(0, strips // 2, unfold, 0)
            if r < strips - 1:
                piece(t, r, (r + 1) * B).wait_recv()

        @pl.when(off_diag)
        def _():
            piece(t, r, 0).wait_recv()

        spot = pl.ds(t * size + r * B, B)
        live_down = down(mask[:, spot].astype(F32))
        moved = jnp.full((B, B), placed[t]) == 1

        def first_pass(c, total):
            at = (t, pl.ds(r * B, B), lanes(c))
            block = jnp.where(moved, recv[at], home[at])
            keep = line + (r * B + shift) <= lane + c * B
            across = live_col[:, pl.ds(pl.multiple_of(t * size + c * B, B), B)]
            block = jnp.where(keep, block, 0.0) * live_down * across
            home[at] = block
            col_acc[t, :, lanes(c)] += folded(block)
            return total + block

        total = lax.fori_loop(0, strips, first_pass, jnp.zeros((B, B), F32))
        row[:, spot] = jnp.sum(total.T, axis=0, keepdims=True)
        corner = home[t, pl.ds(r * B, B), pl.ds(r * B, B)]
        corner = jnp.sum(jnp.where(line == lane, corner, 0.0), axis=0, keepdims=True)
        diag_vec[:, spot] = jnp.where(on_diag, corner, 0.0)
        out_copy(t, r).start()

    u_out[...] = jnp.ones_like(u_out)
    v_out[...] = jnp.ones_like(v_out)
    bias_out[...] = bias[...]
    first_lane = lax.broadcasted_iota(jnp.int32, (1, B), 1)

    def settle(k):
        many = tot.at[k, pl.ds(0, count - 1)]
        pltpu.make_async_copy(many, many, tot_sem.at[k, 0]).wait()
        pltpu.make_async_copy(many, many, tot_sem.at[k, 1]).wait()
        both = jnp.sum(tot[k], axis=0)
        mean = jnp.sum(jnp.where(first_lane == 0, both, 0.0), axis=1, keepdims=True) / jnp.sum(
            jnp.where(first_lane == 1, both, 0.0), axis=1, keepdims=True)
        bias_out[...] = bias_out[...] * jnp.where(mask[...] > 0, sums_now[...] / mean, 1.0)
        u_out[...] = u_out[...] * jnp.where(mask[...] > 0, mean, 1.0)
        v_out[...] = v_out[...] * jnp.where(live_col[...] > 0, mean, 1.0)
        return mean

    for k in range(ITERS):
        if k > 0:
            col_acc[...] = jnp.zeros_like(col_acc)
            for t in range(rows_dev):
                def strip_pass(r, carry):
                    spot = pl.ds(pl.multiple_of(t * size + r * B, B), B)
                    u_down = down(u_out[:, spot])

                    def later_pass(c, total):
                        block = home[t, lanes(r), c * B:(c + 1) * B]
                        col_acc[t, :, c * B:(c + 1) * B] += folded(block * u_down)
                        return total + block * v_out[:, t * size + c * B:t * size + (c + 1) * B]

                    total = jnp.zeros((B, B), F32)
                    for c in range(strips):
                        total = later_pass(c, total)
                    row[:, spot] = jnp.sum(total.T, axis=0, keepdims=True)
                    return carry

                lax.fori_loop(0, strips, strip_pass, 0)
        cols = jnp.concatenate([jnp.sum(col_acc[t], axis=0, keepdims=True) for t in range(rows_dev)], axis=1) * v_out[...]
        rows = row[...] * u_out[...]
        corner = diag_vec[...] * u_out[...] * v_out[...]
        zero = jnp.zeros((1, size), F32)
        moved_cols = jnp.concatenate([zero, cols[:, :width - size]], axis=1)
        mine = rows + jnp.where(on_diag, cols - corner, moved_cols)
        edge = jnp.where(on_diag, 0.0, cols[:, width - size:])
        if k > 0:
            mean = settle(k - 1)
            mine, edge = (jnp.where(value != 0, value * mean * mean, 0.0) for value in (mine, edge))
        contrib[k] = mine
        edge_out[k] = edge
        partial = jnp.sum(mine) + jnp.sum(edge)
        kept = jnp.where(on_diag, jnp.sum(mask[...].astype(F32)), 0.0)
        tot[k, me] = jnp.where(first_lane == 0, partial, jnp.where(first_lane == 1, kept, 0.0))

        def tot_copy(off):
            return pltpu.make_async_remote_copy(
                tot.at[k, me], tot.at[k, me], tot_sem.at[k, 0], tot_sem.at[k, 1], device_id=other(off), device_id_type=MESH)

        def tot_start(off, carry):
            tot_copy(off).start()
            return carry

        to_pair = pltpu.make_async_remote_copy(
            contrib.at[k], pair.at[k], pair_sem.at[k, 0], pair_sem.at[k, 1], device_id=(b, 1 - d), device_id_type=MESH)
        to_edge = [pltpu.make_async_remote_copy(
            edge_out.at[k], edge_in.at[k], edge_sem.at[k, i], edge_sem.at[k, 2],
            device_id=(jnp.minimum(b + 1, n - 1), i), device_id_type=MESH) for i in range(2)]
        to_prev = [pltpu.make_async_remote_copy(
            contrib.at[k, :, :size], nxt.at[k, i], next_sem.at[k, 0], next_sem.at[k, 1 + i],
            device_id=(jnp.maximum(b - 1, 0), 1), device_id_type=MESH) for i in range(2)]

        @pl.when(off_diag & has_next)
        def _():
            for copy in to_edge:
                copy.start()

        for i in range(2):
            @pl.when((d == i) & has_prev)
            def _():
                to_prev[i].start()

        to_pair.start()
        lax.fori_loop(1, count, tot_start, 0)
        to_pair.wait()

        @pl.when(off_diag & has_next)
        def _():
            for copy in to_edge:
                copy.wait_send()
            for copy in to_prev:
                copy.wait_recv()

        @pl.when(has_prev)
        def _():
            to_edge[0].wait_recv()
            to_prev[0].wait_send()

        mine, theirs = contrib[k], pair[k]
        sums = jnp.where(on_diag, mine, theirs) + jnp.where(on_diag, theirs, mine)
        arrived = jnp.where(has_prev, edge_in[k], 0.0)
        if rows_dev > 1:
            arrived = jnp.concatenate([arrived, jnp.zeros((1, width - size), F32)], axis=1)
        sums = sums + arrived
        sums_now[...] = sums
        inverse = 1.0 / jnp.where(mask[...] > 0, sums, 1.0)
        next_sums = nxt[k, 0] + nxt[k, 1] + edge_out[k]
        next_inverse = 1.0 / jnp.where(next_mask[...] > 0, next_sums, 1.0)
        next_inverse = jnp.where(has_next, next_inverse, 0.0)
        if rows_dev > 1:
            next_inverse = jnp.concatenate([inverse[:, size:], next_inverse], axis=1)
        u_out[...] = u_out[...] * inverse
        v_out[...] = v_out[...] * jnp.where(on_diag, inverse, next_inverse)

    settle(ITERS - 1)

    for t, r in order:
        out_copy(t, r).wait()

    @pl.when(on_diag)
    def _():
        for t, r in order:
            if r < strips - 1:
                piece(t, r, (r + 1) * B).wait_send()
        for t in range(rows_dev):
            folds(t).wait_send()

    @pl.when(off_diag)
    def _():
        for t, r in order:
            piece(t, r, 0).wait_send()


def scale(tall, tiles, u, v, bias, out, bias_out):
    bias_out[...] = bias[...]
    for r in range(tall // B):
        spot = pl.ds(r * B, B)
        u_down = jnp.broadcast_to(u[:, spot], (B, B)).T
        for c in range(v.shape[1] // B):
            across = pl.ds(c * B, B)
            out[0, 0, spot, across] = tiles[0, spot, across] * u_down * v[:, across]


def local(n, held_tiles, placed, bin_mask, bias):
    rows_dev, size = held_tiles.shape[0], held_tiles.shape[2]
    strips, width, count = size // B, rows_dev * size, n * 2
    vmem, anywhere = pl.BlockSpec(memory_space=pltpu.VMEM), pl.BlockSpec(memory_space=pl.ANY)
    wide = jax.ShapeDtypeStruct((1, width), F32)
    dma = pltpu.SemaphoreType.DMA
    tiles, u, v, bias_new = pl.pallas_call(
        functools.partial(kernel, n, rows_dev, size),
        out_shape=(jax.ShapeDtypeStruct((rows_dev, size, size), F32), wide, wide, wide),
        in_specs=[anywhere, pl.BlockSpec(memory_space=pltpu.SMEM), vmem, vmem],
        out_specs=(anywhere, vmem, vmem, vmem),
        scratch_shapes=[
            pltpu.VMEM((rows_dev, size, size), F32),
            pltpu.VMEM((rows_dev, size, size), F32),
            pltpu.VMEM((1, width), F32),
            pltpu.VMEM((1, size), jnp.int32),
            pltpu.VMEM((1, width), F32),
            pltpu.VMEM((rows_dev, 8, size), F32),
            pltpu.VMEM((1, width), F32),
            pltpu.VMEM((ITERS, 1, width), F32),
            pltpu.VMEM((ITERS, 1, width), F32),
            pltpu.VMEM((ITERS, 1, size), F32),
            pltpu.VMEM((ITERS, 1, size), F32),
            pltpu.VMEM((ITERS, 2, 1, size), F32),
            pltpu.VMEM((ITERS, count, 1, B), F32),
            pltpu.VMEM((rows_dev, strips // 2, B + 8, B), F32),
            pltpu.VMEM((rows_dev, strips // 2, B + 8, B), F32),
            pltpu.VMEM((1, width), F32),
            dma((rows_dev,)),
            dma((rows_dev, strips)),
            dma((rows_dev, strips)),
            dma((rows_dev, strips)),
            dma((2,)),
            dma((ITERS, 2)),
            dma((ITERS, 3)),
            dma((ITERS, 3)),
            dma((ITERS, 2)),
            dma((rows_dev, 2)),
        ],
        compiler_params=pltpu.CompilerParams(collective_id=0, has_side_effects=True),
    )(held_tiles, placed, bin_mask.reshape(1, width), bias.reshape(1, width))
    tall = 2 * B
    balanced, bias_new = pl.pallas_call(
        functools.partial(scale, tall),
        grid=(rows_dev, size // tall),
        out_shape=(jax.ShapeDtypeStruct((rows_dev, 1, size, size), F32), wide),
        in_specs=[
            pl.BlockSpec((1, tall, size), lambda t, s: (t, s, 0)),
            pl.BlockSpec((1, tall), lambda t, s: (0, t * (size // tall) + s)),
            pl.BlockSpec((1, size), lambda t, s: (0, t)),
            pl.BlockSpec((1, width), lambda t, s: (0, 0)),
        ],
        out_specs=(pl.BlockSpec((1, 1, tall, size), lambda t, s: (t, 0, s, 0)), pl.BlockSpec((1, width), lambda t, s: (0, 0))),
    )(tiles, u, v, bias_new)
    return balanced, bias_new.reshape(width)


def solution(mesh):
    specs = (P("bins", "diag", None, None), P("bins"), P("bins"), P("bins"))
    return jax.shard_map(
        functools.partial(local, mesh.shape["bins"]),
        mesh=mesh,
        in_specs=specs,
        out_specs=(P("bins", "diag", None, None), P("bins")),
        check_vma=False,
    )
```
